32 devices in a mesh: group: 2 (over x), seq: 16 (over z, y, core).
Axes of the slice: x: 2, y: 2, z: 4, core: 2. Of those that a mesh axis runs over, the one named last changes fastest.
Arguments:
- queries: bfloat16 [96, 128, 2560], P(('group', 'seq')), parts along dimension 0, may hold values from -9 to 9
- keys: bfloat16 [96, 128, 2560], P(('group', 'seq')), parts along dimension 0, may hold values from -9 to 9
- values: bfloat16 [96, 128, 2560], P(('group', 'seq')), parts along dimension 0, may hold values from -6 to 6
- block_list: int32 [96, 20, 2], P('group'), parts along dimension 0, may hold values from 0 to 47, as said below
- list_len: int32 [96, 20], P('group'), parts along dimension 0, may hold values from 0 to 2, as said below
- window_time: int32 [20], replicated, may hold values from 0 to 1
- window_rows: int32 [20], replicated, may hold values from 0 to 1
Outputs:
- attention_out: bfloat16 [96, 128, 2560], P(('group', 'seq')), parts along dimension 0
The draws below stay inside these ranges and needn't reach their ends.
There are 2 independent parts, one for each index of `group`. The reference program is written for one: setup_inputs(seed, part) draws one part's arguments, and reference() takes and returns one part's arrays. A program takes and returns all parts, laid end to end along the dimension named above; an argument that names none is the same for every part. Nothing has to cross between parts.
Inputs may be any that keep to these rules, and one draw needn't show every extreme that they name: `block_list`: for the 3 query tiles of one block and one head, all listed tiles lie on a single other block, and together the used entries name exactly 2 distinct tiles; one list's entries are distinct. For the query tiles of one block, no other block holds listed tiles of more than 2 heads, and some block holds those of exactly 2 heads, so the distinct listed pairs of tile and head of one block on another block number at most 4, reached in every draw. Entries of block_list at and after position list_len are not used.
All inputs are finite; a program needn't handle non-finite values.
Results may differ from the reference program's by a relative error of at most 0.0032.
Values may be sent and summed in bfloat16 or wider, within the bound.
No kernel may reach another device: no remote copies, remote signals or barrier semaphores. Data moves between devices by JAX's collectives and lax.ppermute only.
A program may use at most 128 MiB of HBM per device.

```python
import math
import jax
import jax.numpy as jnp
from jax import lax

HEADS = 20
HEAD_DIM = 128
FEAT = 2560
TILE_TOK = 128
TIME_TILES = 1
ROW_TILES = 3
ROW_BLOCKS = 2
LIST = 2
BLOCKS = 16
TILES_DEV = 3
TILES = 48
HEADS_SRC = 2


def draw_queries(key, part):
    inner = jax.random.fold_in(key, 11)
    field = 1.5 * jax.random.truncated_normal(inner, -6.0, 6.0, (TILES, TILE_TOK, FEAT), jnp.float32)
    return field.astype(jnp.bfloat16)


def draw_keys(key, part):
    inner = jax.random.fold_in(key, 13)
    field = 1.5 * jax.random.truncated_normal(inner, -6.0, 6.0, (TILES, TILE_TOK, FEAT), jnp.float32)
    return field.astype(jnp.bfloat16)


def make_lists(key):
    inner = jax.random.fold_in(key, 23)
    keys_all = jax.random.split(inner, 7)
    blocks = jnp.arange(BLOCKS)
    special = jax.random.randint(keys_all[6], (), 0, BLOCKS)
    before = (special + BLOCKS - 1) % BLOCKS
    is_self = blocks[:, None] == blocks[None, :]
    favoured = (blocks[:, None] == special) & (blocks[None, :] == before)
    ranks = jax.vmap(lambda sub: jax.random.permutation(sub, BLOCKS))(jax.random.split(keys_all[0], BLOCKS))
    ranking = jnp.where(is_self, 2 * BLOCKS, 0) + jnp.where(favoured, -BLOCKS, 0) + ranks
    order = jnp.argsort(ranking, axis=1, stable=True)
    group = jnp.arange(HEADS) // HEADS_SRC
    source = order[:, group]
    first = jax.random.randint(keys_all[1], (BLOCKS, HEADS), 0, TILES_DEV)
    stride = jax.random.randint(keys_all[2], (BLOCKS, HEADS), 1, TILES_DEV)
    second = (first + stride) % TILES_DEV
    full_tile = jax.random.randint(keys_all[3], (BLOCKS, HEADS), 0, TILES_DEV)
    lengths = jax.random.randint(keys_all[4], (BLOCKS, TILES_DEV, HEADS), 0, LIST + 1)
    lengths = jnp.where(jnp.arange(TILES_DEV)[None, :, None] == full_tile[:, None, :], LIST, lengths)
    flip = jax.random.randint(keys_all[5], (BLOCKS, TILES_DEV, HEADS), 0, 2)
    one_tile = (source * TILES_DEV + first)[:, None, :]
    other_tile = (source * TILES_DEV + second)[:, None, :]
    entry_first = jnp.where(flip == 1, other_tile, one_tile)
    entry_second = jnp.where(flip == 1, one_tile, other_tile)
    listed = jnp.stack([entry_first, entry_second], axis=-1).reshape(TILES, HEADS, LIST)
    return (listed.astype(jnp.int32), lengths.reshape(TILES, HEADS).astype(jnp.int32))


def draw_block_list(key, part):
    return make_lists(key)[0]


def draw_list_len(key, part):
    return make_lists(key)[1]


def with_ends(values, stream_key, smallest, largest):
    longest = values.shape.index(max(values.shape))
    spots = []
    for shift in (0, 1):
        where = [jax.random.randint(jax.random.fold_in(stream_key, axis), (), 0, length) for axis, length in enumerate(values.shape)]
        where[longest] = (where[longest] + shift) % values.shape[longest]
        spots.append(tuple(where))
    return values.at[spots[0]].set(smallest).at[spots[1]].set(largest)


def block_levels(own_key, shape, pieces, least, high):
    gain, own = 1.0, jax.random.fold_in(own_key, 6)
    for axis_at, blocks in pieces:
        steps = jnp.exp(jax.random.uniform(jax.random.fold_in(own, axis_at), (blocks,), jnp.float32, least / len(pieces), high / len(pieces)))
        gain = gain * jnp.repeat(steps, shape[axis_at] // blocks).reshape([-1 if axis == axis_at else 1 for axis in range(len(shape))])
    return gain


def scatter_about(stream_key, extent, deviation, limit, cuts=(), kind=jnp.bfloat16):
    entries = deviation * jax.random.normal(stream_key, extent, jnp.float32)
    if cuts:
        entries = entries * block_levels(stream_key, extent, cuts, -0.22, 0.18)
    return jnp.clip(entries, -limit, limit).astype(kind)


def setup_inputs(seed: int = 0, part: int = 0) -> dict:
    seeds = jax.random.split(jax.random.key(seed), 8)
    part_splits = jax.random.split(jax.random.fold_in(seeds[7], part), 8)
    return {
        "queries": draw_queries(jax.random.fold_in(jax.random.fold_in(seeds[7], part), 71), part),
        "keys": draw_keys(jax.random.fold_in(jax.random.fold_in(seeds[7], part), 71), part),
        "values": scatter_about(part_splits[2], (TILES, TILE_TOK, FEAT), 1.0, 6.0, ((0, 16),)),
        "block_list": draw_block_list(jax.random.fold_in(jax.random.fold_in(seeds[7], part), 71), part),
        "list_len": draw_list_len(jax.random.fold_in(jax.random.fold_in(seeds[7], part), 71), part),
        "window_time": with_ends(jax.random.randint(seeds[5], (HEADS,), 0, 2), jax.random.fold_in(seeds[5], 1), 0, 1).astype(jnp.int32),
        "window_rows": with_ends(jax.random.randint(seeds[6], (HEADS,), 0, 2), jax.random.fold_in(seeds[6], 1), 0, 1).astype(jnp.int32),
    }


BIG_NEG = -1e+30

def tile_coords(ids):
    block = ids // TILES_DEV
    local = ids % TILES_DEV
    time_pos = block // ROW_BLOCKS * TIME_TILES + local // ROW_TILES
    row_pos = block % ROW_BLOCKS * ROW_TILES + local % ROW_TILES
    return (time_pos, row_pos)

def tile_number(time_pos, row_pos):
    block = time_pos // TIME_TILES * ROW_BLOCKS + row_pos // ROW_TILES
    local = time_pos % TIME_TILES * ROW_TILES + row_pos % ROW_TILES
    return (block * TILES_DEV + local).astype(jnp.int32)

def reference(queries, keys, values, block_list, list_len, window_time, window_rows):
    time_count = TIME_TILES * BLOCKS // ROW_BLOCKS
    row_count = ROW_BLOCKS * ROW_TILES
    ids = jnp.arange(TILES, dtype=jnp.int32)
    time_pos, row_pos = tile_coords(ids)
    step_time = jnp.array([-1, -1, -1, 0, 0, 0, 1, 1, 1], jnp.int32)
    step_row = jnp.array([-1, 0, 1, -1, 0, 1, -1, 0, 1], jnp.int32)
    near_time = time_pos[:, None] + step_time[None, :]
    near_row = row_pos[:, None] + step_row[None, :]
    inside = (near_time >= 0) & (near_time < time_count) & (near_row >= 0) & (near_row < row_count)
    near_ids = tile_number(jnp.clip(near_time, 0, time_count - 1), jnp.clip(near_row, 0, row_count - 1))
    live = jnp.arange(LIST, dtype=jnp.int32)[None, None, :] < list_len[:, :, None]
    scale = 1.0 / math.sqrt(HEAD_DIM)

    def one_head(head):
        q_head = lax.dynamic_slice_in_dim(queries, head * HEAD_DIM, HEAD_DIM, 2)
        k_head = lax.dynamic_slice_in_dim(keys, head * HEAD_DIM, HEAD_DIM, 2)
        v_head = lax.dynamic_slice_in_dim(values, head * HEAD_DIM, HEAD_DIM, 2)
        far_ids = lax.dynamic_index_in_dim(block_list, head, 1, keepdims=False)
        key_rows = jnp.concatenate([k_head[near_ids].reshape(TILES, 9 * TILE_TOK, HEAD_DIM), k_head[far_ids].reshape(TILES, LIST * TILE_TOK, HEAD_DIM)], axis=1)
        value_rows = jnp.concatenate([v_head[near_ids].reshape(TILES, 9 * TILE_TOK, HEAD_DIM), v_head[far_ids].reshape(TILES, LIST * TILE_TOK, HEAD_DIM)], axis=1)
        scores = jnp.einsum('txd,tyd->txy', q_head.astype(jnp.float32), key_rows.astype(jnp.float32)) * scale
        win_ok = inside & (jnp.abs(step_time)[None, :] <= window_time[head]) & (jnp.abs(step_row)[None, :] <= window_rows[head])
        list_ok = lax.dynamic_index_in_dim(live, head, 1, keepdims=False)
        usable = jnp.concatenate([jnp.repeat(win_ok, TILE_TOK, axis=1), jnp.repeat(list_ok, TILE_TOK, axis=1)], axis=1)
        scores = jnp.where(usable[:, None, :], scores, BIG_NEG)
        top = lax.optimization_barrier(jnp.max(scores, axis=2, keepdims=True))
        weights = jnp.exp(scores - top)
        total = lax.optimization_barrier(jnp.sum(weights, axis=2, keepdims=True))
        rounded = lax.optimization_barrier(weights.astype(jnp.bfloat16))
        mixed = jnp.einsum('txy,tyd->txd', rounded.astype(jnp.float32), value_rows.astype(jnp.float32))
        return (mixed / total).astype(jnp.bfloat16)
    results = lax.map(one_head, jnp.arange(HEADS, dtype=jnp.int32))
    return jnp.transpose(results, (1, 2, 0, 3)).reshape(TILES, TILE_TOK, FEAT)
```

```python
import functools
import math

import jax
import jax.numpy as jnp
from jax import lax
from jax.experimental import pallas as pl
from jax.experimental.pallas import tpu as pltpu
from jax.sharding import PartitionSpec as P

TIME_TILES = 1
ROW_TILES = 3
ROW_BLOCKS = 2
LIST = 2
BIG_NEG = -1e30
BIG_INT = 1 << 20


def relay_fits(mesh):
    where = mesh.devices[0]
    chips = [getattr(dev, "coords", None) for dev in where[::ROW_BLOCKS]]
    if any(c is None for c in chips) or len(chips) % 2:
        return False

    def gap(a, b):
        return sum(abs(p - q) for p, q in zip(chips[a], chips[b]))

    count = len(chips)
    return (
        all(gap(t, t + 1) == 1 for t in range(0, count, 2))
        and all(gap(t, t + 1) == 2 for t in range(1, count - 1, 2))
        and all(gap(t, t + 2) == 1 for t in range(count - 2))
    )


def column(head, width):
    return pl.ds(pl.multiple_of(head * width, width), width)


def pack_halo_kernel(head_of, place, key_hbm, val_hbm, halo, edge, kbuf, vbuf, sem_in, sem_out):
    cap = halo.shape[0]
    width = halo.shape[-1]
    loads = [
        pltpu.make_async_copy(key_hbm, kbuf, sem_in.at[0]),
        pltpu.make_async_copy(val_hbm, vbuf, sem_in.at[1]),
    ]
    for load in loads:
        load.start()
    side = place[0]
    for part, buf in enumerate((kbuf, vbuf)):
        loads[part].wait()
        pltpu.make_async_copy(buf.at[side], edge.at[part], sem_out.at[1]).start()

        @pl.loop(0, cap)
        def _(slot):
            pltpu.make_async_copy(
                buf.at[:, :, column(head_of[slot], width)], halo.at[slot, part], sem_out.at[0]
            ).start()

    pltpu.make_async_copy(halo, halo, sem_out.at[0]).wait()
    pltpu.make_async_copy(edge, edge, sem_out.at[1]).wait()


def pack_far_kernel(code, key_hbm, val_hbm, far, kbuf, vbuf, sem_in, sem_out):
    blocks, _, slots, _, width = far.shape
    loads = [
        pltpu.make_async_copy(key_hbm, kbuf, sem_in.at[0]),
        pltpu.make_async_copy(val_hbm, vbuf, sem_in.at[1]),
    ]
    for load in loads:
        load.start()
    for part, buf in enumerate((kbuf, vbuf)):
        loads[part].wait()

        @pl.loop(0, blocks)
        def _(dest):
            for rank in range(slots // LIST):
                word = code[dest, rank]
                head = word // 16
                for which, tile in enumerate((word // 4 % 4, word % 4)):
                    pltpu.make_async_copy(
                        buf.at[tile, :, column(head, width)],
                        far.at[dest, part, rank * LIST + which],
                        sem_out,
                    ).start()

    pltpu.make_async_copy(far, far, sem_out).wait()


def scores_of(query, keys):
    return lax.dot_general(
        query, keys, (((1,), (1,)), ((), ())), preferred_element_type=jnp.float32
    )


def near_kernel(
    slot, kind, place, q_ref, k_ref, v_ref, edge_ref, n1_ref, n2_ref, e1_ref, e2_ref,
    acc_ref, top_ref, sum_ref, *, factor
):
    head = pl.program_id(0)
    tiles, tile_len, _ = q_ref.shape
    neg = jnp.float32(BIG_NEG)
    zero = jnp.float32(0)
    first_bias = jnp.where(place[1] == 1, zero, neg)
    last_bias = jnp.where(place[1] == 0, zero, neg)
    time_bias = (None, jnp.where(place[2] > 0, zero, neg), jnp.where(place[3] > 0, zero, neg))
    lanes = lax.broadcasted_iota(jnp.int32, (tile_len, top_ref.shape[-1]), 1)

    def own(part, u, along):
        if along == 0:
            return (k_ref, v_ref)[part][u]
        return (n1_ref, n2_ref)[along - 1][0, part, u]

    def side(part, along):
        if along == 0:
            return edge_ref[part]
        return (e1_ref, e2_ref)[along - 1][0, part]

    def run(times, rows):
        for u in range(tiles):
            pieces = []
            for along in range(3 if times else 1):
                bias = time_bias[along]
                if not rows:
                    pieces.append((own(0, u, along), own(1, u, along), bias))
                    continue
                for w in (u - 1, u, u + 1):
                    if 0 <= w < tiles:
                        pieces.append((own(0, w, along), own(1, w, along), bias))
                    else:
                        edge_bias = first_bias if w < 0 else last_bias
                        if bias is not None:
                            edge_bias = edge_bias + bias
                        pieces.append((side(0, along), side(1, along), edge_bias))
            query = q_ref[u]
            raw = scores_of(query, jnp.concatenate([p[0] for p in pieces], axis=0))
            blocks = []
            for at, (_, _, bias) in enumerate(pieces):
                block = raw[:, at * tile_len : (at + 1) * tile_len]
                blocks.append(block if bias is None else block + bias)
            best = functools.reduce(jnp.maximum, blocks)
            top = jnp.max(best, axis=1, keepdims=True)
            shift = top * factor
            weights = [jnp.exp2(block * factor - shift) for block in blocks]
            total = jnp.sum(functools.reduce(jnp.add, weights), axis=1, keepdims=True)
            rounded = jnp.concatenate([w.astype(jnp.bfloat16) for w in weights], axis=1)
            mixed = jnp.dot(
                rounded,
                jnp.concatenate([p[1] for p in pieces], axis=0),
                preferred_element_type=jnp.float32,
            )
            acc_ref[u] = mixed
            top_ref[u] = jnp.where(lanes == head, top, top_ref[u])
            sum_ref[u] = jnp.where(lanes == head, total, sum_ref[u])

    for times in (0, 1):
        for rows in (0, 1):
            pl.when(kind[head] == times + 2 * rows)(functools.partial(run, times, rows))


def far_kernel(
    source, rank, bits, q_ref, acc_ref, top_ref, sum_ref, far_ref, out_ref, *, factor
):
    head = pl.program_id(0)
    tiles, tile_len, width = q_ref.shape
    neg = jnp.float32(BIG_NEG)
    zero = jnp.float32(0)
    lanes = lax.broadcasted_iota(jnp.int32, (tile_len, top_ref.shape[-1]), 1)
    keys = far_ref[0, 0].reshape(LIST * tile_len, width)
    vals = far_ref[0, 1].reshape(LIST * tile_len, width)
    raw_all = scores_of(q_ref[...].reshape(tiles * tile_len, width), keys)
    word = bits[head]
    for u in range(tiles):
        blocks = []
        for which in range(LIST):
            live = (word // (1 << (u * LIST + which))) % 2
            block = raw_all[
                u * tile_len : (u + 1) * tile_len, which * tile_len : (which + 1) * tile_len
            ]
            blocks.append(block + jnp.where(live > 0, zero, neg))
        near_top = jnp.sum(jnp.where(lanes == head, top_ref[u], zero), axis=1, keepdims=True)
        near_sum = jnp.sum(jnp.where(lanes == head, sum_ref[u], zero), axis=1, keepdims=True)
        best = functools.reduce(jnp.maximum, blocks)
        top = jnp.maximum(near_top, jnp.max(best, axis=1, keepdims=True))
        shift = top * factor
        weights = [jnp.exp2(block * factor - shift) for block in blocks]
        keep = jnp.exp2(near_top * factor - shift)
        total = keep * near_sum + jnp.sum(
            functools.reduce(jnp.add, weights), axis=1, keepdims=True
        )
        mixed = jnp.dot(
            jnp.concatenate([w.astype(jnp.bfloat16) for w in weights], axis=1),
            vals,
            preferred_element_type=jnp.float32,
        )
        out_ref[u] = ((acc_ref[u] * keep + mixed) / total).astype(out_ref.dtype)


def any_spec():
    return pl.BlockSpec(memory_space=pl.ANY)


def smem_spec():
    return pl.BlockSpec(memory_space=pltpu.SMEM)


def on_device(relay, queries, keys, values, block_list, list_len, window_time, window_rows):
    tiles, tile_len, feat = queries.shape
    heads = window_time.shape[0]
    width = feat // heads
    blocks = lax.axis_size("seq")
    device = lax.axis_index("seq").astype(jnp.int32)
    time_block = device // ROW_BLOCKS
    row_pos = device % ROW_BLOCKS
    time_blocks = blocks // ROW_BLOCKS
    dtype = keys.dtype
    factor = math.log2(math.e) / math.sqrt(width)
    head_ids = jnp.arange(heads, dtype=jnp.int32)
    below = (head_ids[:, None] < head_ids[None, :]).astype(jnp.int32)

    timed = (window_time > 0).astype(jnp.int32)
    before = jnp.sum(timed[:, None] * below, axis=0)
    timed_count = jnp.sum(timed)
    slot = jnp.maximum(before + timed - 1, 0)
    head_of = jnp.sum(
        jnp.where((before[None, :] == head_ids[:, None]) & (timed[None, :] > 0), head_ids, 0),
        axis=1,
    )
    kind = timed + 2 * (window_rows > 0).astype(jnp.int32)
    side = jnp.where(row_pos == 0, tiles - 1, 0)
    if relay:
        first_ok = jnp.int32(1)
        second_ok = jnp.where(
            time_block % 2 == 0, time_block > 0, time_block < time_blocks - 1
        ).astype(jnp.int32)
    else:
        first_ok = (time_block > 0).astype(jnp.int32)
        second_ok = (time_block < time_blocks - 1).astype(jnp.int32)
    place = jnp.stack([side, row_pos, first_ok, second_ok]).astype(jnp.int32)

    low = high = None
    for entry in range(LIST):
        live = list_len > entry
        item = block_list[:, :, entry]
        small, large = jnp.where(live, item, BIG_INT), jnp.where(live, item, -1)
        low = small if low is None else jnp.minimum(low, small)
        high = large if high is None else jnp.maximum(high, large)
    low = jnp.min(low.reshape(blocks, tiles, heads), axis=1)
    high = jnp.max(high.reshape(blocks, tiles, heads), axis=1)
    source_all = low // tiles
    per_source = (heads + blocks - 2) // (blocks - 1)
    want = (source_all == device).astype(jnp.int32)
    want_rank = jnp.sum(want[:, :, None] * below[None], axis=1)
    code_all = head_ids[None, :] * 16 + (low % tiles) * 4 + high % tiles
    code = jnp.stack(
        [
            jnp.sum(jnp.where((want > 0) & (want_rank == r), code_all, 0), axis=1)
            for r in range(per_source)
        ],
        axis=1,
    )
    own_low = lax.dynamic_index_in_dim(low, device, 0, keepdims=False)
    own_high = lax.dynamic_index_in_dim(high, device, 0, keepdims=False)
    source = own_low // tiles
    rank = jnp.sum((source[:, None] == source[None, :]).astype(jnp.int32) * below, axis=0)
    own_list = lax.dynamic_slice_in_dim(block_list, device * tiles, tiles, 0)
    own_len = lax.dynamic_slice_in_dim(list_len, device * tiles, tiles, 0)
    bits = jnp.zeros((heads,), jnp.int32)
    for u in range(tiles):
        for which, target in enumerate((own_low, own_high)):
            hit = jnp.zeros((heads,), bool)
            for entry in range(LIST):
                hit |= (own_list[u, :, entry] == target) & (own_len[u] > entry)
            bits += hit.astype(jnp.int32) << (u * LIST + which)

    kv_scratch = [
        pltpu.VMEM(keys.shape, dtype),
        pltpu.VMEM(values.shape, dtype),
        pltpu.SemaphoreType.DMA((2,)),
    ]
    slots = per_source * LIST
    far_shape = (blocks, 2, slots, tile_len, width)
    pair_tile = tile_len * width * 2

    def pack_far():
        return pl.pallas_call(
            pack_far_kernel,
            out_shape=jax.ShapeDtypeStruct(far_shape, dtype),
            in_specs=[smem_spec(), any_spec(), any_spec()],
            out_specs=any_spec(),
            scratch_shapes=kv_scratch + [pltpu.SemaphoreType.DMA],
            cost_estimate=pl.CostEstimate(
                flops=0, transcendentals=0, bytes_accessed=2 * blocks * slots * pair_tile
            ),
            name="pack_far",
        )(code, keys, values)

    pair_route = [(i, i ^ 1) for i in range(blocks)]

    def permute(value, route):
        return lax.ppermute(value, "seq", route)

    def near(cap):
        halo, edge = pl.pallas_call(
            pack_halo_kernel,
            out_shape=(
                jax.ShapeDtypeStruct((cap, 2, tiles, tile_len, width), dtype),
                jax.ShapeDtypeStruct((2, tile_len, feat), dtype),
            ),
            in_specs=[smem_spec(), smem_spec(), any_spec(), any_spec()],
            out_specs=(any_spec(), any_spec()),
            scratch_shapes=kv_scratch + [pltpu.SemaphoreType.DMA((2,))],
            cost_estimate=pl.CostEstimate(
                flops=0, transcendentals=0, bytes_accessed=cap * 6 * pair_tile
            ),
            name="pack_halo",
        )(head_of, place, keys, values)

        def split(value):
            return lax.dynamic_index_in_dim(value, side, 2, keepdims=False)

        if relay:
            step = 2 * ROW_BLOCKS
            swap = [(i, i ^ ROW_BLOCKS) for i in range(blocks)]
            shift = []
            for i in range(blocks):
                to = i + step if (i // ROW_BLOCKS) % 2 == 0 else i - step
                if 0 <= to < blocks:
                    shift.append((i, to))
            first = permute(halo, swap)
            second = permute(first, shift)
        else:
            step = ROW_BLOCKS
            first = permute(halo, [(i, i + step) for i in range(blocks - step)])
            second = permute(halo, [(i + step, i) for i in range(blocks - step)])
        far = lax.all_to_all(pack_far(), "seq", split_axis=0, concat_axis=0, tiled=True)
        edge = permute(edge, pair_route)
        edge_first = permute(split(first), pair_route)
        edge_second = permute(split(second), pair_route)

        def at_head(h, *_):
            return (0, 0, h)

        def at_slot(h, slot_ref, *_):
            return (slot_ref[h], 0, 0, 0, 0)

        def at_slot_edge(h, slot_ref, *_):
            return (slot_ref[h], 0, 0, 0)

        tile_spec = pl.BlockSpec((tiles, tile_len, width), at_head)
        stat_spec = pl.BlockSpec((tiles, tile_len, 128), lambda h, *_: (0, 0, 0))
        halo_spec = pl.BlockSpec((1, 2, tiles, tile_len, width), at_slot)
        halo_edge_spec = pl.BlockSpec((1, 2, tile_len, width), at_slot_edge)
        pairs = heads * tiles * 6
        acc, top, total = pl.pallas_call(
            functools.partial(near_kernel, factor=factor),
            grid_spec=pltpu.PrefetchScalarGridSpec(
                num_scalar_prefetch=3,
                grid=(heads,),
                in_specs=[
                    tile_spec,
                    tile_spec,
                    tile_spec,
                    pl.BlockSpec((2, tile_len, width), at_head),
                    halo_spec,
                    halo_spec,
                    halo_edge_spec,
                    halo_edge_spec,
                ],
                out_specs=[tile_spec, stat_spec, stat_spec],
            ),
            out_shape=(
                jax.ShapeDtypeStruct((tiles, tile_len, feat), jnp.float32),
                jax.ShapeDtypeStruct((tiles, tile_len, 128), jnp.float32),
                jax.ShapeDtypeStruct((tiles, tile_len, 128), jnp.float32),
            ),
            cost_estimate=pl.CostEstimate(
                flops=pairs * 4 * tile_len * tile_len * width,
                transcendentals=pairs * tile_len * tile_len,
                bytes_accessed=8 * tiles * tile_len * feat * 2,
            ),
            name="near",
        )(slot, kind, place, queries, keys, values, edge, first, second, edge_first, edge_second)
        return acc, top, total, far

    caps = [c for c in (6, 8, 10, 12, 14) if c < heads] + [heads]
    pick = sum((timed_count > c).astype(jnp.int32) for c in caps[:-1])
    acc, top, total, far = lax.switch(pick, [functools.partial(near, c) for c in caps])

    def at_head(h, *_):
        return (0, 0, h)

    tile_spec = pl.BlockSpec((tiles, tile_len, width), at_head)
    stat_spec = pl.BlockSpec((tiles, tile_len, 128), lambda h, *_: (0, 0, 0))
    return pl.pallas_call(
        functools.partial(far_kernel, factor=factor),
        grid_spec=pltpu.PrefetchScalarGridSpec(
            num_scalar_prefetch=3,
            grid=(heads,),
            in_specs=[
                tile_spec,
                tile_spec,
                stat_spec,
                stat_spec,
                pl.BlockSpec(
                    (1, 2, LIST, tile_len, width), lambda h, src, rk, *_: (src[h], 0, rk[h], 0, 0)
                ),
            ],
            out_specs=tile_spec,
        ),
        out_shape=jax.ShapeDtypeStruct(queries.shape, queries.dtype),
        cost_estimate=pl.CostEstimate(
            flops=heads * tiles * LIST * 4 * tile_len * tile_len * width,
            transcendentals=heads * tiles * LIST * tile_len * tile_len,
            bytes_accessed=6 * tiles * tile_len * feat * 2,
        ),
        name="far",
    )(source, rank, bits, queries, acc, top, total, far)


def solution(mesh):
    return jax.shard_map(
        functools.partial(on_device, relay_fits(mesh)),
        mesh=mesh,
        in_specs=(
            P(("group", "seq"), None, None),
            P(("group", "seq"), None, None),
            P(("group", "seq"), None, None),
            P("group", None, None),
            P("group", None),
            P(),
            P(),
        ),
        out_specs=P(("group", "seq"), None, None),
        check_vma=False,
    )
```

```python
import functools
import math

import jax
import jax.numpy as jnp
from jax import lax
from jax.experimental import pallas as pl
from jax.experimental.pallas import tpu as pltpu
from jax.sharding import PartitionSpec as P


ROW_BLOCKS = 2
LIST = 2
BIG_NEG = -1e30
BIG_INT = 1 << 20

CAPS = (7, 9, 11, 13)


def relay_fits(mesh):
    where = mesh.devices[0]
    chips = [getattr(dev, "coords", None) for dev in where[::ROW_BLOCKS]]
    if any(c is None for c in chips) or len(chips) % 2:
        return False

    def gap(a, b):
        return sum(abs(p - q) for p, q in zip(chips[a], chips[b]))

    count = len(chips)
    return (
        all(gap(t, t + 1) == 1 for t in range(0, count, 2))
        and all(gap(t, t + 1) == 2 for t in range(1, count - 1, 2))
        and all(gap(t, t + 2) == 1 for t in range(count - 2))
    )


def column(head, width):
    return pl.ds(pl.multiple_of(head * width, width), width)


def pack_kernel(
    timed, device, lists, lens, lists_s, lens_s, key_hbm, val_hbm,
    halo_key, halo_val, edge, far, plan, kbuf, vbuf, span, words, code, sem_in, sem_out, sem_code
):
    heads = timed.shape[0]
    tiles = kbuf.shape[0]
    cap = halo_key.shape[0]
    blocks, _, slots, _, width = far.shape
    me = device[0]
    base = me * tiles
    loads = [
        pltpu.make_async_copy(key_hbm, kbuf, sem_in.at[0]),
        pltpu.make_async_copy(val_hbm, vbuf, sem_in.at[1]),
    ]
    for load in loads:
        load.start()

    span[...] = jnp.zeros_like(span)
    low = high = None
    for entry in range(LIST):
        live = lens[...] > entry
        item = lists[:, entry, :]
        small, large = jnp.where(live, item, BIG_INT), jnp.where(live, item, -1)
        low = small if low is None else jnp.minimum(low, small)
        high = large if high is None else jnp.maximum(high, large)
    span[0, :heads, : low.shape[1]] = low
    span[1, :heads, : low.shape[1]] = high
    lanes = span.shape[2]
    low = low_in = span[0]
    high = high_in = span[1]
    for u in range(1, tiles):
        low = jnp.minimum(low, pltpu.roll(low_in, lanes - u, 1))
        high = jnp.maximum(high, pltpu.roll(high_in, lanes - u, 1))
    rows = lax.broadcasted_iota(jnp.int32, low.shape, 0)
    want = (low >= base) & (low < base + tiles) & (rows < heads)
    count = low.shape[0]
    under = lax.broadcasted_iota(jnp.int32, (count, count), 1) < lax.broadcasted_iota(
        jnp.int32, (count, count), 0
    )
    order = jnp.dot(
        jnp.where(under, 1.0, 0.0), jnp.where(want, 1.0, 0.0), preferred_element_type=jnp.float32
    )
    word = rows * 16 + (low - base) * 4 + (high - base)
    for r in range(slots // LIST):
        chosen = want & (order > r - 0.5) & (order < r + 0.5)
        words[r : r + 1, :] = jnp.sum(jnp.where(chosen, word, 0), axis=0, keepdims=True)
    to_scalar = pltpu.make_async_copy(words, code, sem_code)
    to_scalar.start()

    def note(h, found):
        @pl.when(timed[h] > 0)
        def _():
            plan[3, found] = h

        return found + jnp.where(timed[h] > 0, 1, 0)

    found = lax.fori_loop(0, heads, note, jnp.int32(0))
    plan[4, 0] = found
    last = jnp.where(found > 0, plan[3, jnp.maximum(found - 1, 0)], 0)

    @pl.loop(0, cap)
    def _(slot):
        @pl.when(slot >= found)
        def _():
            plan[3, slot] = last

    side = jnp.where(me % ROW_BLOCKS == 0, tiles - 1, 0)
    bufs = (kbuf, vbuf)
    for part, halo in enumerate((halo_key, halo_val)):
        loads[part].wait()
        pltpu.make_async_copy(bufs[part].at[side], edge.at[part], sem_out.at[2]).start()

        @pl.loop(0, cap)
        def _(slot):
            pltpu.make_async_copy(
                bufs[part].at[:, :, column(plan[3, slot], width)], halo.at[slot], sem_out.at[part]
            ).start()

    to_scalar.wait()

    @pl.loop(0, blocks)
    def _(dest):
        for r in range(slots // LIST):
            item = code[r, dest * tiles]
            for part in range(2):
                for which, tile in enumerate((item // 4 % 4, item % 4)):
                    pltpu.make_async_copy(
                        bufs[part].at[tile, :, column(item // 16, width)],
                        far.at[dest, part, r * LIST + which],
                        sem_out.at[3],
                    ).start()

    @pl.loop(0, blocks)
    def _(b):
        plan[5, b] = 0

    @pl.loop(0, heads)
    def _(h):
        small = jnp.int32(BIG_INT)
        large = jnp.int32(-1)
        got = []
        for u in range(tiles):
            for entry in range(LIST):
                live = lens_s[h, base + u] > entry
                item = jnp.where(live, lists_s[h, entry, base + u], -1)
                got.append((u, item))
                small = jnp.where(live, jnp.minimum(small, item), small)
                large = jnp.maximum(large, item)
        bits = jnp.int32(0)
        for u, item in got:
            bits |= jnp.where(item == small, 1 << (u * LIST), 0)
            bits |= jnp.where(item == large, 2 << (u * LIST), 0)
        owner = small // tiles
        plan[0, h] = owner
        plan[1, h] = plan[5, owner]
        plan[2, h] = bits
        plan[5, owner] = plan[5, owner] + 1

    pltpu.make_async_copy(halo_key, halo_key, sem_out.at[0]).wait()
    pltpu.make_async_copy(halo_val, halo_val, sem_out.at[1]).wait()
    pltpu.make_async_copy(edge, edge, sem_out.at[2]).wait()
    pltpu.make_async_copy(far, far, sem_out.at[3]).wait()


def scores_of(query, keys):
    return lax.dot_general(
        query, keys, (((1,), (1,)), ((), ())), preferred_element_type=jnp.float32
    )


def with_ones(vals):
    return jnp.concatenate([vals, jnp.ones_like(vals)], axis=1)


def around(u, rows):
    return [u] if not rows else [u - 1, u, u + 1]


def softmax_step(blocks, vals, old, factor):
    width = vals.shape[1]
    top = jnp.max(functools.reduce(jnp.maximum, blocks), axis=1, keepdims=True)
    if old is not None:
        top = jnp.maximum(old[1], top)
    else:
        top = jnp.broadcast_to(top, (blocks[0].shape[0], width))
    shift = top * factor
    weights = [jnp.exp2(block * factor - shift).astype(jnp.bfloat16) for block in blocks]
    both = jnp.dot(
        jnp.concatenate(weights, axis=1), with_ones(vals), preferred_element_type=jnp.float32
    )
    mixed, total = both[:, :width], both[:, width:]
    if old is not None:
        keep = jnp.exp2(old[1] * factor - shift)
        mixed = old[0] * keep + mixed
        total = old[2] * keep + total
    return mixed, top, total


def window_kernel(keys, vals, edge_key, edge_val, q_ref, old, new, rows, row_pos, factor):
    tiles, tile_len, _ = q_ref.shape
    neg, zero = jnp.float32(BIG_NEG), jnp.float32(0)
    for u in range(tiles):
        pieces = []
        for w in around(u, rows):
            if 0 <= w < tiles:
                pieces.append((keys(w), vals(w), None))
            else:
                on = row_pos == (1 if w < 0 else 0)
                pieces.append((edge_key(), edge_val(), jnp.where(on, zero, neg)))
        raw = scores_of(q_ref[u], jnp.concatenate([p[0] for p in pieces], axis=0))
        blocks = []
        for at, (_, _, bias) in enumerate(pieces):
            block = raw[:, at * tile_len : (at + 1) * tile_len]
            blocks.append(block if bias is None else block + bias)
        state = None if old is None else [ref[u] for ref in old]
        result = softmax_step(
            blocks, jnp.concatenate([p[1] for p in pieces], axis=0), state, factor
        )
        for ref, value in zip(new, result):
            ref[u] = value


def local_kernel(reach, device, q_ref, k_ref, v_ref, edge_ref, *new, factor):
    head = pl.program_id(0)
    row_pos = device[0] % ROW_BLOCKS
    for rows in (0, 1):

        @pl.when((reach[head] > 0) == bool(rows))
        def _():
            window_kernel(
                lambda w: k_ref[w],
                lambda w: v_ref[w],
                lambda: edge_ref[0],
                lambda: edge_ref[1],
                q_ref, None, new, rows, row_pos, factor,
            )


def time_kernel(
    plan, reach, device, valid, q_ref, k_ref, v_ref, edge_ref, *refs, factor
):
    old, new = refs[:3], refs[3:]
    slot = pl.program_id(0)
    head = plan[3, slot]
    row_pos = device[0] % ROW_BLOCKS
    go = (slot < plan[4, 0]) & (valid[0] > 0)
    for rows in (0, 1):

        @pl.when(go & ((reach[head] > 0) == bool(rows)))
        def _():
            window_kernel(
                lambda w: k_ref[0, w],
                lambda w: v_ref[0, w],
                lambda: edge_ref[0, 0],
                lambda: edge_ref[1, 0],
                q_ref, old, new, rows, row_pos, factor,
            )

    @pl.when((slot < plan[4, 0]) & (valid[0] == 0) | (slot == 0) & (plan[4, 0] == 0))
    def _():
        for before, after in zip(old, new):
            after[...] = before[...]


def far_kernel(plan, q_ref, acc_ref, top_ref, sum_ref, *refs, factor):
    fars, out_ref = refs[:-1], refs[-1]
    step = pl.program_id(0)
    tiles, tile_len, _ = q_ref.shape
    width = fars[0].shape[-1]
    neg, zero = jnp.float32(BIG_NEG), jnp.float32(0)
    for g, far_ref in enumerate(fars):
        at = slice(g * width, (g + 1) * width)
        word = plan[2, step * len(fars) + g]
        keys = far_ref[0, 0].reshape(LIST * tile_len, width)
        vals = far_ref[0, 1].reshape(LIST * tile_len, width)
        for u in range(tiles):
            raw = scores_of(q_ref[u, :, at], keys)
            blocks = []
            for which in range(LIST):
                live = (word // (1 << (u * LIST + which))) % 2
                block = raw[:, which * tile_len : (which + 1) * tile_len]
                blocks.append(block + jnp.where(live > 0, zero, neg))
            state = (acc_ref[u, :, at], top_ref[u, :, at], sum_ref[u, :, at])
            mixed, _, total = softmax_step(blocks, vals, state, factor)
            out_ref[u, :, at] = (mixed / total).astype(out_ref.dtype)


def any_spec():
    return pl.BlockSpec(memory_space=pl.ANY)


def smem_spec():
    return pl.BlockSpec(memory_space=pltpu.SMEM)


def vmem_spec():
    return pl.BlockSpec(memory_space=pltpu.VMEM)


def on_device(relay, queries, keys, values, block_list, list_len, window_time, window_rows):
    tiles, tile_len, feat = queries.shape
    heads = window_time.shape[0]
    width = feat // heads
    blocks = lax.axis_size("seq")
    axis = lax.axis_index("seq").astype(jnp.int32)
    device = axis.reshape(1)
    time_block = axis // ROW_BLOCKS
    row_pos = axis % ROW_BLOCKS
    time_blocks = blocks // ROW_BLOCKS
    dtype = keys.dtype
    factor = math.log2(math.e) / math.sqrt(width)
    timed_count = jnp.sum((window_time > 0).astype(jnp.int32))
    side = jnp.where(row_pos == 0, tiles - 1, 0)
    if relay:
        first_ok = jnp.int32(1)
        second_ok = jnp.where(time_block % 2 == 0, time_block > 0, time_block < time_blocks - 1)
    else:
        first_ok = time_block > 0
        second_ok = time_block < time_blocks - 1
    oks = [ok.astype(jnp.int32).reshape(1) for ok in (first_ok, second_ok)]
    lists = jnp.transpose(block_list, (1, 2, 0))
    lens = jnp.transpose(list_len, (1, 0))
    per_source = (heads + blocks - 2) // (blocks - 1)
    slots = per_source * LIST
    pair_tile = tile_len * width * 2
    lanes = -(-lists.shape[2] // 128) * 128
    sublanes = -(-heads // 8) * 8
    pair_route = [(i, i ^ 1) for i in range(blocks)]

    def permute(value, route):
        return lax.ppermute(value, "seq", route)

    def at_head(h, *_):
        return (0, 0, h)

    state_shape = [jax.ShapeDtypeStruct((tiles, tile_len, feat), jnp.float32)] * 3
    tile_spec = pl.BlockSpec((tiles, tile_len, width), at_head)

    def near(cap):
        return near_of(cap)

    def near_of(cap):
        halo_shape = jax.ShapeDtypeStruct((cap, tiles, tile_len, width), dtype)
        halo_key, halo_val, edge, far, plan = pl.pallas_call(
            pack_kernel,
            out_shape=(
                halo_shape,
                halo_shape,
                jax.ShapeDtypeStruct((2, tile_len, feat), dtype),
                jax.ShapeDtypeStruct((blocks, 2, slots, tile_len, width), dtype),
                jax.ShapeDtypeStruct((8, 128), jnp.int32),
            ),
            in_specs=[smem_spec(), smem_spec(), vmem_spec(), vmem_spec(), smem_spec(), smem_spec()]
            + [any_spec()] * 2,
            out_specs=[any_spec()] * 4 + [smem_spec()],
            scratch_shapes=[
                pltpu.VMEM(keys.shape, dtype),
                pltpu.VMEM(values.shape, dtype),
                pltpu.VMEM((2, sublanes, lanes), jnp.int32),
                pltpu.VMEM((8, lanes), jnp.int32),
                pltpu.SMEM((8, lanes), jnp.int32),
                pltpu.SemaphoreType.DMA((2,)),
                pltpu.SemaphoreType.DMA((4,)),
                pltpu.SemaphoreType.DMA,
            ],
            cost_estimate=pl.CostEstimate(
                flops=0,
                transcendentals=0,
                bytes_accessed=(2 * blocks * slots + 6 * cap) * pair_tile,
            ),
            name="pack",
        )(window_time, device, lists, lens, lists, lens, keys, values)

        if relay:
            step = 2 * ROW_BLOCKS
            one_hop = [(i, i ^ ROW_BLOCKS) for i in range(blocks)]
            other = []
            for i in range(blocks):
                to = i + step if (i // ROW_BLOCKS) % 2 == 0 else i - step
                if 0 <= to < blocks:
                    other.append((i, to))
            straight = []
            for i in range(blocks):
                to = i - ROW_BLOCKS if (i // ROW_BLOCKS) % 2 == 0 else i + ROW_BLOCKS
                if 0 <= to < blocks:
                    straight.append((i, to))
            first_key = permute(halo_key, one_hop)
            first_val = permute(halo_val, one_hop)
            first = [first_key, first_val]
            second_key = permute(first_key, other)
            second_val = permute(halo_val, straight)
            second = [second_key, second_val]
        else:
            step = ROW_BLOCKS
            after = [(i, i + step) for i in range(blocks - step)]
            ahead = [(i + step, i) for i in range(blocks - step)]
            first_key = permute(halo_key, after)
            first_val = permute(halo_val, after)
            first = [first_key, first_val]
            second_key = permute(halo_key, ahead)
            second_val = permute(halo_val, ahead)
            second = [second_key, second_val]
        far = lax.all_to_all(far, "seq", split_axis=0, concat_axis=0, tiled=True)
        edge = permute(edge, pair_route)

        pairs = heads * tiles * 3
        state = pl.pallas_call(
            functools.partial(local_kernel, factor=factor),
            grid_spec=pltpu.PrefetchScalarGridSpec(
                num_scalar_prefetch=2,
                grid=(heads,),
                in_specs=[tile_spec] * 3 + [pl.BlockSpec((2, tile_len, width), at_head)],
                out_specs=[tile_spec] * 3,
            ),
            out_shape=state_shape,
            cost_estimate=pl.CostEstimate(
                flops=pairs * 4 * tile_len * tile_len * width,
                transcendentals=pairs * tile_len * tile_len,
                bytes_accessed=10 * tiles * tile_len * feat * 2,
            ),
            name="local",
        )(window_rows, device, queries, keys, values, edge)

        def at_plan(s, plan_ref, *_):
            return (0, 0, plan_ref[3, s])

        planned = pl.BlockSpec((tiles, tile_len, width), at_plan)
        pairs = cap * tiles * 3
        for halo, ok in zip((first, second), oks):
            sides = jnp.stack([lax.dynamic_index_in_dim(x, side, 1, keepdims=False) for x in halo])
            sides = permute(sides, pair_route)
            halo_spec = pl.BlockSpec((1, tiles, tile_len, width), lambda s, *_: (s, 0, 0, 0))
            state = pl.pallas_call(
                functools.partial(time_kernel, factor=factor),
                grid_spec=pltpu.PrefetchScalarGridSpec(
                    num_scalar_prefetch=4,
                    grid=(cap,),
                    in_specs=[
                        planned,
                        halo_spec,
                        halo_spec,
                        pl.BlockSpec((2, 1, tile_len, width), lambda s, *_: (0, s, 0, 0)),
                        planned,
                        planned,
                        planned,
                    ],
                    out_specs=[planned] * 3,
                ),
                out_shape=state_shape,
                input_output_aliases={8: 0, 9: 1, 10: 2},
                cost_estimate=pl.CostEstimate(
                    flops=pairs * 4 * tile_len * tile_len * width,
                    transcendentals=pairs * tile_len * tile_len,
                    bytes_accessed=16 * cap * tiles * pair_tile,
                ),
                name="time",
            )(plan, window_rows, device, ok, queries, halo[0], halo[1], sides, *state)
        return (*state, far, plan)

    caps = [c for c in CAPS if c < heads] + [heads]
    pick = sum((timed_count > c).astype(jnp.int32) for c in caps[:-1])
    *state, far, plan = lax.switch(pick, [functools.partial(near, c) for c in caps])

    group = 2 if heads % 2 == 0 else 1
    wide_spec = pl.BlockSpec((tiles, tile_len, width * group), at_head)

    def far_spec(g):
        return pl.BlockSpec(
            (1, 2, LIST, tile_len, width),
            lambda h, plan_ref: (plan_ref[0, h * group + g], 0, plan_ref[1, h * group + g], 0, 0),
        )

    return pl.pallas_call(
        functools.partial(far_kernel, factor=factor),
        grid_spec=pltpu.PrefetchScalarGridSpec(
            num_scalar_prefetch=1,
            grid=(heads // group,),
            in_specs=[wide_spec] * 4 + [far_spec(g) for g in range(group)],
            out_specs=wide_spec,
        ),
        out_shape=jax.ShapeDtypeStruct(queries.shape, queries.dtype),
        cost_estimate=pl.CostEstimate(
            flops=heads * tiles * LIST * 4 * tile_len * tile_len * width,
            transcendentals=heads * tiles * LIST * tile_len * tile_len,
            bytes_accessed=10 * tiles * tile_len * feat * 2,
        ),
        name="far",
    )(plan, queries, *state, *([far] * group))


def solution(mesh):
    return jax.shard_map(
            functools.partial(on_device, relay_fits(mesh)),
            mesh=mesh,
            in_specs=(
                P(("group", "seq"), None, None),
                P(("group", "seq"), None, None),
                P(("group", "seq"), None, None),
                P("group", None, None),
                P("group", None),
                P(),
                P(),
            ),
            out_specs=P(("group", "seq"), None, None),
            check_vma=False,
    )
```

```python
import functools
import math

import jax
import jax.numpy as jnp
from jax import lax
from jax.experimental import pallas as pl
from jax.experimental.pallas import tpu as pltpu
from jax.sharding import PartitionSpec as P


ROW_BLOCKS = 2
LIST = 2
BIG_NEG = -1e30
BIG_INT = 1 << 20

CAPS = (6, 8, 10, 12, 14)
GROUP = 2


def relay_fits(mesh):
    where = mesh.devices[0]
    chips = [getattr(dev, "coords", None) for dev in where[::ROW_BLOCKS]]
    if any(c is None for c in chips) or len(chips) % 2:
        return False

    def gap(a, b):
        return sum(abs(p - q) for p, q in zip(chips[a], chips[b]))

    count = len(chips)
    return (
        all(gap(t, t + 1) == 1 for t in range(0, count, 2))
        and all(gap(t, t + 1) == 2 for t in range(1, count - 1, 2))
        and all(gap(t, t + 2) == 1 for t in range(count - 2))
    )


def column(head, width):
    return pl.ds(pl.multiple_of(head * width, width), width)


def pack_kernel(
    timed, device, lists, lens, lists_s, lens_s, key_hbm, val_hbm,
    halo_key, halo_val, edge, far, plan, kbuf, vbuf, span, words, code, sem_in, sem_out, sem_code
):
    heads = timed.shape[0]
    tiles = kbuf.shape[0]
    cap = halo_key.shape[0]
    blocks, _, slots, _, width = far.shape
    me = device[0]
    base = me * tiles
    loads = [
        pltpu.make_async_copy(key_hbm, kbuf, sem_in.at[0]),
        pltpu.make_async_copy(val_hbm, vbuf, sem_in.at[1]),
    ]
    for load in loads:
        load.start()

    span[...] = jnp.zeros_like(span)
    low = high = None
    for entry in range(LIST):
        live = lens[...] > entry
        item = lists[:, entry, :]
        small, large = jnp.where(live, item, BIG_INT), jnp.where(live, item, -1)
        low = small if low is None else jnp.minimum(low, small)
        high = large if high is None else jnp.maximum(high, large)
    span[0, :heads, : low.shape[1]] = low
    span[1, :heads, : low.shape[1]] = high
    lanes = span.shape[2]
    low = low_in = span[0]
    high = high_in = span[1]
    for u in range(1, tiles):
        low = jnp.minimum(low, pltpu.roll(low_in, lanes - u, 1))
        high = jnp.maximum(high, pltpu.roll(high_in, lanes - u, 1))
    rows = lax.broadcasted_iota(jnp.int32, low.shape, 0)
    want = (low >= base) & (low < base + tiles) & (rows < heads)
    count = low.shape[0]
    under = lax.broadcasted_iota(jnp.int32, (count, count), 1) < lax.broadcasted_iota(
        jnp.int32, (count, count), 0
    )
    order = jnp.dot(
        jnp.where(under, 1.0, 0.0), jnp.where(want, 1.0, 0.0), preferred_element_type=jnp.float32
    )
    word = rows * 16 + (low - base) * 4 + (high - base)
    for r in range(slots // LIST):
        chosen = want & (order > r - 0.5) & (order < r + 0.5)
        words[r : r + 1, :] = jnp.sum(jnp.where(chosen, word, 0), axis=0, keepdims=True)
    to_scalar = pltpu.make_async_copy(words, code, sem_code)
    to_scalar.start()

    def note(h, found):
        @pl.when(timed[h] > 0)
        def _():
            plan[3, found] = h

        after = found + jnp.where(timed[h] > 0, 1, 0)
        plan[6, h] = jnp.maximum(after - 1, 0)
        plan[7, h] = timed[h]
        return after

    found = lax.fori_loop(0, heads, note, jnp.int32(0))
    plan[4, 0] = found
    last = jnp.where(found > 0, plan[3, jnp.maximum(found - 1, 0)], 0)

    @pl.loop(0, cap)
    def _(slot):
        @pl.when(slot >= found)
        def _():
            plan[3, slot] = last

    side = jnp.where(me % ROW_BLOCKS == 0, tiles - 1, 0)
    bufs = (kbuf, vbuf)
    for part, halo in enumerate((halo_key, halo_val)):
        loads[part].wait()
        pltpu.make_async_copy(bufs[part].at[side], edge.at[part], sem_out.at[2]).start()

        @pl.loop(0, cap)
        def _(slot):
            pltpu.make_async_copy(
                bufs[part].at[:, :, column(plan[3, slot], width)], halo.at[slot], sem_out.at[part]
            ).start()

    to_scalar.wait()

    @pl.loop(0, blocks)
    def _(dest):
        for r in range(slots // LIST):
            item = code[r, dest * tiles]
            for part in range(2):
                for which, tile in enumerate((item // 4 % 4, item % 4)):
                    pltpu.make_async_copy(
                        bufs[part].at[tile, :, column(item // 16, width)],
                        far.at[dest, part, r * LIST + which],
                        sem_out.at[3],
                    ).start()

    @pl.loop(0, blocks)
    def _(b):
        plan[5, b] = 0

    @pl.loop(0, heads)
    def _(h):
        small = jnp.int32(BIG_INT)
        large = jnp.int32(-1)
        got = []
        for u in range(tiles):
            for entry in range(LIST):
                live = lens_s[h, base + u] > entry
                item = jnp.where(live, lists_s[h, entry, base + u], -1)
                got.append((u, item))
                small = jnp.where(live, jnp.minimum(small, item), small)
                large = jnp.maximum(large, item)
        bits = jnp.int32(0)
        for u, item in got:
            bits |= jnp.where(item == small, 1 << (u * LIST), 0)
            bits |= jnp.where(item == large, 2 << (u * LIST), 0)
        owner = small // tiles
        plan[0, h] = owner
        plan[1, h] = plan[5, owner]
        plan[2, h] = bits
        plan[5, owner] = plan[5, owner] + 1

    pltpu.make_async_copy(halo_key, halo_key, sem_out.at[0]).wait()
    pltpu.make_async_copy(halo_val, halo_val, sem_out.at[1]).wait()
    pltpu.make_async_copy(edge, edge, sem_out.at[2]).wait()
    pltpu.make_async_copy(far, far, sem_out.at[3]).wait()


def scores_of(query, keys):
    return lax.dot_general(
        query, keys, (((1,), (1,)), ((), ())), preferred_element_type=jnp.float32
    )


def window_blocks(sources, rows, q_ref, at, row_pos):
    tiles, tile_len = q_ref.shape[:2]
    neg, zero = jnp.float32(BIG_NEG), jnp.float32(0)
    if not rows:
        blocks = []
        for u in range(tiles):
            raw = scores_of(q_ref[u, :, at], jnp.concatenate([k(u) for k, _ in sources], axis=0))
            blocks.append([raw[:, i * tile_len : (i + 1) * tile_len] for i in range(len(sources))])
        return blocks, [[v(u) for _, v in sources] for u in range(tiles)]
    query = jnp.concatenate([q_ref[u, :, at] for u in range(tiles)], axis=0)
    keys = [k(w) for k, _ in sources for w in range(tiles + 1)]
    vals = [v(w) for _, v in sources for w in range(tiles + 1)]
    raw = scores_of(query, jnp.concatenate(keys, axis=0))
    blocks = []
    for u in range(tiles):
        line = []
        for i in range(len(keys)):
            w = i % (tiles + 1)
            block = raw[u * tile_len : (u + 1) * tile_len, i * tile_len : (i + 1) * tile_len]
            if w == tiles:
                sides = [side for side, end in ((1, 0), (0, tiles - 1)) if u == end]
                if not sides:
                    block = None
                else:
                    block = block + jnp.where(row_pos == sides[0], zero, neg)
            elif abs(w - u) > 1:
                block = None
            line.append(block)
        blocks.append(line)
    return blocks, vals


def weights_of(line, old_top, factor):
    live = [block for block in line if block is not None]
    top = jnp.max(functools.reduce(jnp.maximum, live), axis=1, keepdims=True)
    if old_top is not None:
        top = jnp.maximum(old_top, top)
    shift = top * factor
    weights = [None if b is None else jnp.exp2(b * factor - shift) for b in line]
    total = functools.reduce(jnp.add, [w for w in weights if w is not None])
    total = jnp.sum(total, axis=1, keepdims=True)
    blank = jnp.zeros(live[0].shape, jnp.bfloat16)
    rounded = [blank if w is None else w.astype(jnp.bfloat16) for w in weights]
    return top, total, jnp.concatenate(rounded, axis=1)


def product(weights, vals):
    return jnp.dot(weights, jnp.concatenate(vals, axis=0), preferred_element_type=jnp.float32)


def near_kernel(
    plan, reach, device, valid, q_ref, k_ref, v_ref, edge_ref, hk_ref, hv_ref, side_ref,
    acc_ref, top_ref, sum_ref, *, factor
):
    head = pl.program_id(0)
    tiles, tile_len, _ = q_ref.shape
    row_pos = device[0] % ROW_BLOCKS
    lanes = lax.broadcasted_iota(jnp.int32, (tile_len, top_ref.shape[-1]), 1)
    local = (
        lambda w: k_ref[w] if w < tiles else edge_ref[0],
        lambda w: v_ref[w] if w < tiles else edge_ref[1],
    )
    timed = (
        lambda w: hk_ref[0, w] if w < tiles else side_ref[0, 0],
        lambda w: hv_ref[0, w] if w < tiles else side_ref[1, 0],
    )

    def run(sources, rows):
        blocks, vals = window_blocks(sources, rows, q_ref, slice(None), row_pos)
        parts = [weights_of(line, None, factor) for line in blocks]
        if rows:
            mixed = product(jnp.concatenate([p[2] for p in parts], axis=0), vals)
            mixed = [mixed[u * tile_len : (u + 1) * tile_len] for u in range(tiles)]
        else:
            mixed = [product(parts[u][2], vals[u]) for u in range(tiles)]
        for u in range(tiles):
            acc_ref[u] = mixed[u]
            top_ref[u] = jnp.where(lanes == head, parts[u][0], top_ref[u])
            sum_ref[u] = jnp.where(lanes == head, parts[u][1], sum_ref[u])

    with_time = (plan[7, head] > 0) & (valid[0] > 0)
    for rows in (0, 1):
        for time in (0, 1):
            pl.when((with_time == bool(time)) & ((reach[head] > 0) == bool(rows)))(
                functools.partial(run, (local, timed) if time else (local,), rows)
            )


def column_of(ref, u, lanes, head):
    return jnp.sum(jnp.where(lanes == head, ref[u], jnp.float32(0)), axis=1, keepdims=True)


def time_kernel(
    plan, reach, device, valid, q_ref, hk_ref, hv_ref, side_ref, acc_ref, top_ref, sum_ref,
    before_ref, out_ref, *, factor
):
    slot = pl.program_id(0)
    head = plan[3, slot]
    tiles, tile_len, _ = q_ref.shape
    row_pos = device[0] % ROW_BLOCKS
    lanes = lax.broadcasted_iota(jnp.int32, (tile_len, top_ref.shape[-1]), 1)
    source = (
        lambda w: hk_ref[0, w] if w < tiles else side_ref[0, 0],
        lambda w: hv_ref[0, w] if w < tiles else side_ref[1, 0],
    )

    def run(rows):
        blocks, vals = window_blocks((source,), rows, q_ref, slice(None), row_pos)
        tops = [column_of(top_ref, u, lanes, head) for u in range(tiles)]
        parts = [weights_of(blocks[u], tops[u], factor) for u in range(tiles)]
        if rows:
            mixed = product(jnp.concatenate([p[2] for p in parts], axis=0), vals)
            mixed = [mixed[u * tile_len : (u + 1) * tile_len] for u in range(tiles)]
        else:
            mixed = [product(parts[u][2], vals[u]) for u in range(tiles)]
        for u in range(tiles):
            top, total, _ = parts[u]
            keep = jnp.exp2(tops[u] * factor - top * factor)
            total = keep * column_of(sum_ref, u, lanes, head) + total
            out_ref[u] = ((acc_ref[u] * keep + mixed[u]) / total).astype(out_ref.dtype)

    count = plan[4, 0]
    go = (slot < count) & (valid[0] > 0)
    for rows in (0, 1):
        pl.when(go & ((reach[head] > 0) == bool(rows)))(functools.partial(run, rows))

    @pl.when(jnp.logical_not(go) & ((slot < count) | (slot == 0)))
    def _():
        out_ref[...] = before_ref[...]


def far_kernel(plan, q_ref, acc_ref, top_ref, sum_ref, *refs, factor):
    fars, (out_ref, acc_out, top_out, sum_out) = refs[:-4], refs[-4:]
    step = pl.program_id(0)
    tiles, tile_len, _ = q_ref.shape
    width = out_ref.shape[-1] // len(fars)
    neg, zero = jnp.float32(BIG_NEG), jnp.float32(0)
    lanes = lax.broadcasted_iota(jnp.int32, (tile_len, top_ref.shape[-1]), 1)
    for g, far_ref in enumerate(fars):
        head = step * len(fars) + g
        at = slice(g * width, (g + 1) * width)
        word = plan[2, head]
        query = jnp.concatenate([q_ref[u, :, at] for u in range(tiles)], axis=0)
        raw = scores_of(query, jnp.concatenate([far_ref[0, 0, i] for i in range(LIST)], axis=0))
        lines = []
        for u in range(tiles):
            line = []
            for i in range(LIST):
                live = (word // (1 << (u * LIST + i))) % 2
                block = raw[u * tile_len : (u + 1) * tile_len, i * tile_len : (i + 1) * tile_len]
                line.append(block + jnp.where(live > 0, zero, neg))
            lines.append(line)
        tops = [column_of(top_ref, u, lanes, head) for u in range(tiles)]
        parts = [weights_of(lines[u], tops[u], factor) for u in range(tiles)]
        mixed = product(
            jnp.concatenate([p[2] for p in parts], axis=0), [far_ref[0, 1, i] for i in range(LIST)]
        )
        for u in range(tiles):
            top, total, _ = parts[u]
            keep = jnp.exp2(tops[u] * factor - top * factor)
            total = keep * column_of(sum_ref, u, lanes, head) + total
            whole = acc_ref[u, :, at] * keep + mixed[u * tile_len : (u + 1) * tile_len]
            out_ref[u, :, at] = (whole / total).astype(out_ref.dtype)
            acc_out[u, :, at] = whole
            top_out[u] = jnp.where(lanes == head, top, top_out[u])
            sum_out[u] = jnp.where(lanes == head, total, sum_out[u])


def any_spec():
    return pl.BlockSpec(memory_space=pl.ANY)


def smem_spec():
    return pl.BlockSpec(memory_space=pltpu.SMEM)


def vmem_spec():
    return pl.BlockSpec(memory_space=pltpu.VMEM)


def on_device(relay, queries, keys, values, block_list, list_len, window_time, window_rows):
    tiles, tile_len, feat = queries.shape
    heads = window_time.shape[0]
    width = feat // heads
    blocks = lax.axis_size("seq")
    axis = lax.axis_index("seq").astype(jnp.int32)
    device = axis.reshape(1)
    time_block = axis // ROW_BLOCKS
    row_pos = axis % ROW_BLOCKS
    time_blocks = blocks // ROW_BLOCKS
    dtype = keys.dtype
    factor = math.log2(math.e) / math.sqrt(width)
    timed_count = jnp.sum((window_time > 0).astype(jnp.int32))
    side = jnp.where(row_pos == 0, tiles - 1, 0)
    if relay:
        first_ok = jnp.int32(1)
        second_ok = jnp.where(time_block % 2 == 0, time_block > 0, time_block < time_blocks - 1)
    else:
        first_ok = time_block > 0
        second_ok = time_block < time_blocks - 1
    oks = [ok.astype(jnp.int32).reshape(1) for ok in (first_ok, second_ok)]
    lists = jnp.transpose(block_list, (1, 2, 0))
    lens = jnp.transpose(list_len, (1, 0))
    per_source = (heads + blocks - 2) // (blocks - 1)
    slots = per_source * LIST
    pair_tile = tile_len * width * 2
    lanes = -(-lists.shape[2] // 128) * 128
    sublanes = -(-heads // 8) * 8
    pair_route = [(i, i ^ 1) for i in range(blocks)]

    def permute(value, route):
        return lax.ppermute(value, "seq", route)

    def at_head(h, *_):
        return (0, 0, h)

    tile_spec = pl.BlockSpec((tiles, tile_len, width), at_head)

    def near(cap):
        return near_of(cap)

    def near_of(cap):
        halo_shape = jax.ShapeDtypeStruct((cap, tiles, tile_len, width), dtype)
        halo_key, halo_val, edge, far, plan = pl.pallas_call(
            pack_kernel,
            out_shape=(
                halo_shape,
                halo_shape,
                jax.ShapeDtypeStruct((2, tile_len, feat), dtype),
                jax.ShapeDtypeStruct((blocks, 2, slots, tile_len, width), dtype),
                jax.ShapeDtypeStruct((8, 128), jnp.int32),
            ),
            in_specs=[smem_spec(), smem_spec(), vmem_spec(), vmem_spec(), smem_spec(), smem_spec()]
            + [any_spec()] * 2,
            out_specs=[any_spec()] * 4 + [smem_spec()],
            scratch_shapes=[
                pltpu.VMEM(keys.shape, dtype),
                pltpu.VMEM(values.shape, dtype),
                pltpu.VMEM((2, sublanes, lanes), jnp.int32),
                pltpu.VMEM((8, lanes), jnp.int32),
                pltpu.SMEM((8, lanes), jnp.int32),
                pltpu.SemaphoreType.DMA((2,)),
                pltpu.SemaphoreType.DMA((4,)),
                pltpu.SemaphoreType.DMA,
            ],
            cost_estimate=pl.CostEstimate(
                flops=0,
                transcendentals=0,
                bytes_accessed=(2 * blocks * slots + 6 * cap) * pair_tile,
            ),
            name="pack",
        )(window_time, device, lists, lens, lists, lens, keys, values)

        if relay:
            step = 2 * ROW_BLOCKS
            one_hop = [(i, i ^ ROW_BLOCKS) for i in range(blocks)]
            other = []
            for i in range(blocks):
                to = i + step if (i // ROW_BLOCKS) % 2 == 0 else i - step
                if 0 <= to < blocks:
                    other.append((i, to))
            straight = []
            for i in range(blocks):
                to = i - ROW_BLOCKS if (i // ROW_BLOCKS) % 2 == 0 else i + ROW_BLOCKS
                if 0 <= to < blocks:
                    straight.append((i, to))
            first_key = permute(halo_key, one_hop)
            first_val = permute(halo_val, one_hop)
            first = [first_key, first_val]
            second_key = permute(first_key, other)
            second_val = permute(halo_val, straight)
            second = [second_key, second_val]
        else:
            step = ROW_BLOCKS
            after = [(i, i + step) for i in range(blocks - step)]
            ahead = [(i + step, i) for i in range(blocks - step)]
            first_key = permute(halo_key, after)
            first_val = permute(halo_val, after)
            first = [first_key, first_val]
            second_key = permute(halo_key, ahead)
            second_val = permute(halo_val, ahead)
            second = [second_key, second_val]
        far = lax.all_to_all(far, "seq", split_axis=0, concat_axis=0, tiled=True)
        edge = permute(edge, pair_route)

        halves = []
        for halo in (first, second):
            sides = jnp.stack(
                [lax.dynamic_index_in_dim(x, side, 1, keepdims=False) for x in halo]
            )
            halves.append((halo[0], halo[1], permute(sides, pair_route)))

        def halo_specs(at):
            block = (1, tiles, tile_len, width)
            return [
                pl.BlockSpec(block, lambda s, plan_ref, *_: (plan_ref[6, at(s)], 0, 0, 0)),
                pl.BlockSpec(block, lambda s, plan_ref, *_: (plan_ref[6, at(s)], 0, 0, 0)),
                pl.BlockSpec(
                    (2, 1, tile_len, width), lambda s, plan_ref, *_: (0, plan_ref[6, at(s)], 0, 0)
                ),
            ]

        stat_spec = pl.BlockSpec((tiles, tile_len, 128), lambda h, *_: (0, 0, 0))
        stat_shape = jax.ShapeDtypeStruct((tiles, tile_len, 128), jnp.float32)
        pairs = (heads + cap) * tiles * 2
        state = pl.pallas_call(
            functools.partial(near_kernel, factor=factor),
            grid_spec=pltpu.PrefetchScalarGridSpec(
                num_scalar_prefetch=4,
                grid=(heads,),
                in_specs=[tile_spec] * 3
                + [pl.BlockSpec((2, tile_len, width), at_head)]
                + halo_specs(lambda s: s),
                out_specs=[tile_spec, stat_spec, stat_spec],
            ),
            out_shape=(
                jax.ShapeDtypeStruct((tiles, tile_len, feat), jnp.float32),
                stat_shape,
                stat_shape,
            ),
            cost_estimate=pl.CostEstimate(
                flops=pairs * 4 * tile_len * tile_len * width,
                transcendentals=pairs * tile_len * tile_len,
                bytes_accessed=8 * tiles * tile_len * feat * 2,
            ),
            name="near",
        )(plan, window_rows, device, oks[0], queries, keys, values, edge, *halves[0])

        group = GROUP if heads % GROUP == 0 else 1
        wide_spec = pl.BlockSpec((tiles, tile_len, width * group), at_head)

        def far_spec(g):
            return pl.BlockSpec(
                (1, 2, LIST, tile_len, width),
                lambda s, p: (p[0, s * group + g], 0, p[1, s * group + g], 0, 0),
            )

        acc_shape = jax.ShapeDtypeStruct((tiles, tile_len, feat), jnp.float32)
        pairs = heads * tiles * LIST
        out, *state = pl.pallas_call(
            functools.partial(far_kernel, factor=factor),
            grid_spec=pltpu.PrefetchScalarGridSpec(
                num_scalar_prefetch=1,
                grid=(heads // group,),
                in_specs=[wide_spec] * 2
                + [stat_spec] * 2
                + [far_spec(g) for g in range(group)],
                out_specs=[wide_spec] * 2 + [stat_spec] * 2,
            ),
            out_shape=(
                jax.ShapeDtypeStruct(queries.shape, queries.dtype),
                acc_shape,
                stat_shape,
                stat_shape,
            ),
            cost_estimate=pl.CostEstimate(
                flops=pairs * 4 * tile_len * tile_len * width,
                transcendentals=pairs * tile_len * tile_len,
                bytes_accessed=8 * tiles * tile_len * feat * 2,
            ),
            name="far",
        )(plan, queries, *state, *([far] * group))

        def at_plan(s, plan_ref, *_):
            return (0, 0, plan_ref[3, s])

        planned = pl.BlockSpec((tiles, tile_len, width), at_plan)
        halo_spec = pl.BlockSpec((1, tiles, tile_len, width), lambda s, *_: (s, 0, 0, 0))
        pairs = cap * tiles * 3
        return pl.pallas_call(
            functools.partial(time_kernel, factor=factor),
            grid_spec=pltpu.PrefetchScalarGridSpec(
                num_scalar_prefetch=4,
                grid=(cap,),
                in_specs=[
                    planned,
                    halo_spec,
                    halo_spec,
                    pl.BlockSpec((2, 1, tile_len, width), lambda s, *_: (0, s, 0, 0)),
                    planned,
                    stat_spec,
                    stat_spec,
                    planned,
                ],
                out_specs=planned,
            ),
            out_shape=jax.ShapeDtypeStruct(queries.shape, queries.dtype),
            input_output_aliases={11: 0},
            cost_estimate=pl.CostEstimate(
                flops=pairs * 4 * tile_len * tile_len * width,
                transcendentals=pairs * tile_len * tile_len,
                bytes_accessed=8 * cap * tiles * pair_tile,
            ),
            name="time",
        )(plan, window_rows, device, oks[1], queries, *halves[1], *state, out)

    caps = [c for c in CAPS if c < heads] + [heads]
    pick = sum((timed_count > c).astype(jnp.int32) for c in caps[:-1])
    return lax.switch(pick, [functools.partial(near, c) for c in caps])


def solution(mesh):
    return jax.shard_map(
            functools.partial(on_device, relay_fits(mesh)),
            mesh=mesh,
            in_specs=(
                P(("group", "seq"), None, None),
                P(("group", "seq"), None, None),
                P(("group", "seq"), None, None),
                P("group", None, None),
                P("group", None),
                P(),
                P(),
            ),
            out_specs=P(("group", "seq"), None, None),
            check_vma=False,
    )
```

```python
import functools
import math

import jax
import jax.numpy as jnp
from jax import lax
from jax.experimental import pallas as pl
from jax.experimental.pallas import tpu as pltpu
from jax.sharding import PartitionSpec as P


ROW_BLOCKS = 2
LIST = 2
BIG_NEG = -1e30
BIG_INT = 1 << 20

CAPS = (8, 10, 12, 14, 17)
GROUP = 2


def relay_fits(mesh):
    where = mesh.devices[0]
    chips = [getattr(dev, "coords", None) for dev in where[::ROW_BLOCKS]]
    if any(c is None for c in chips) or len(chips) % 2:
        return False

    def gap(a, b):
        return sum(abs(p - q) for p, q in zip(chips[a], chips[b]))

    count = len(chips)
    return (
        all(gap(t, t + 1) == 1 for t in range(0, count, 2))
        and all(gap(t, t + 1) == 2 for t in range(1, count - 1, 2))
        and all(gap(t, t + 2) == 1 for t in range(count - 2))
    )


def column(head, width):
    return pl.ds(pl.multiple_of(head * width, width), width)


def pack_kernel(
    timed, device, lists, lens, lists_s, lens_s, key_hbm, val_hbm,
    halo_key, halo_val, edge, far, plan, kbuf, vbuf, span, words, code, sem_in, sem_out, sem_code
):
    heads = timed.shape[0]
    tiles = kbuf.shape[0]
    cap = halo_key.shape[0]
    blocks, _, slots, _, width = far.shape
    me = device[0]
    base = me * tiles
    loads = [
        pltpu.make_async_copy(key_hbm, kbuf, sem_in.at[0]),
        pltpu.make_async_copy(val_hbm, vbuf, sem_in.at[1]),
    ]
    for load in loads:
        load.start()

    span[...] = jnp.zeros_like(span)
    low = high = None
    for entry in range(LIST):
        live = lens[...] > entry
        item = lists[:, entry, :]
        small, large = jnp.where(live, item, BIG_INT), jnp.where(live, item, -1)
        low = small if low is None else jnp.minimum(low, small)
        high = large if high is None else jnp.maximum(high, large)
    span[0, :heads, : low.shape[1]] = low
    span[1, :heads, : low.shape[1]] = high
    lanes = span.shape[2]
    low = low_in = span[0]
    high = high_in = span[1]
    for u in range(1, tiles):
        low = jnp.minimum(low, pltpu.roll(low_in, lanes - u, 1))
        high = jnp.maximum(high, pltpu.roll(high_in, lanes - u, 1))
    rows = lax.broadcasted_iota(jnp.int32, low.shape, 0)
    want = (low >= base) & (low < base + tiles) & (rows < heads)
    count = low.shape[0]
    under = lax.broadcasted_iota(jnp.int32, (count, count), 1) < lax.broadcasted_iota(
        jnp.int32, (count, count), 0
    )
    order = jnp.dot(
        jnp.where(under, 1.0, 0.0), jnp.where(want, 1.0, 0.0), preferred_element_type=jnp.float32
    )
    word = rows * 16 + (low - base) * 4 + (high - base)
    for r in range(slots // LIST):
        chosen = want & (order > r - 0.5) & (order < r + 0.5)
        words[r : r + 1, :] = jnp.sum(jnp.where(chosen, word, 0), axis=0, keepdims=True)
    to_scalar = pltpu.make_async_copy(words, code, sem_code)
    to_scalar.start()

    def note(h, found):
        @pl.when(timed[h] > 0)
        def _():
            plan[3, found] = h

        after = found + jnp.where(timed[h] > 0, 1, 0)
        plan[6, h] = jnp.maximum(after - 1, 0)
        plan[7, h] = timed[h]
        return after

    found = lax.fori_loop(0, heads, note, jnp.int32(0))
    plan[4, 0] = found
    last = jnp.where(found > 0, plan[3, jnp.maximum(found - 1, 0)], 0)

    @pl.loop(0, cap)
    def _(slot):
        @pl.when(slot >= found)
        def _():
            plan[3, slot] = last

    side = jnp.where(me % ROW_BLOCKS == 0, tiles - 1, 0)
    bufs = (kbuf, vbuf)
    for part, halo in enumerate((halo_key, halo_val)):
        loads[part].wait()
        pltpu.make_async_copy(bufs[part].at[side], edge.at[part], sem_out.at[2]).start()

        @pl.loop(0, cap)
        def _(slot):
            pltpu.make_async_copy(
                bufs[part].at[:, :, column(plan[3, slot], width)], halo.at[slot], sem_out.at[part]
            ).start()

    to_scalar.wait()

    @pl.loop(0, blocks)
    def _(dest):
        for r in range(slots // LIST):
            item = code[r, dest * tiles]
            for part in range(2):
                for which, tile in enumerate((item // 4 % 4, item % 4)):
                    pltpu.make_async_copy(
                        bufs[part].at[tile, :, column(item // 16, width)],
                        far.at[dest, part, r * LIST + which],
                        sem_out.at[3],
                    ).start()

    @pl.loop(0, blocks)
    def _(b):
        plan[5, b] = 0

    @pl.loop(0, heads)
    def _(h):
        small = jnp.int32(BIG_INT)
        large = jnp.int32(-1)
        got = []
        for u in range(tiles):
            for entry in range(LIST):
                live = lens_s[h, base + u] > entry
                item = jnp.where(live, lists_s[h, entry, base + u], -1)
                got.append((u, item))
                small = jnp.where(live, jnp.minimum(small, item), small)
                large = jnp.maximum(large, item)
        bits = jnp.int32(0)
        for u, item in got:
            bits |= jnp.where(item == small, 1 << (u * LIST), 0)
            bits |= jnp.where(item == large, 2 << (u * LIST), 0)
        owner = small // tiles
        plan[0, h] = owner
        plan[1, h] = plan[5, owner]
        plan[2, h] = bits
        plan[5, owner] = plan[5, owner] + 1

    pltpu.make_async_copy(halo_key, halo_key, sem_out.at[0]).wait()
    pltpu.make_async_copy(halo_val, halo_val, sem_out.at[1]).wait()
    pltpu.make_async_copy(edge, edge, sem_out.at[2]).wait()
    pltpu.make_async_copy(far, far, sem_out.at[3]).wait()


def scores_of(query, keys):
    return lax.dot_general(
        query, keys, (((1,), (1,)), ((), ())), preferred_element_type=jnp.float32
    )


def window_blocks(sources, rows, q_ref, at, row_pos):
    tiles, tile_len = q_ref.shape[:2]
    neg, zero = jnp.float32(BIG_NEG), jnp.float32(0)
    if not rows:
        blocks = []
        for u in range(tiles):
            raw = scores_of(q_ref[u, :, at], jnp.concatenate([k(u) for k, _ in sources], axis=0))
            blocks.append([raw[:, i * tile_len : (i + 1) * tile_len] for i in range(len(sources))])
        return blocks, [[v(u) for _, v in sources] for u in range(tiles)]
    query = jnp.concatenate([q_ref[u, :, at] for u in range(tiles)], axis=0)
    keys = [k(w) for k, _ in sources for w in range(tiles + 1)]
    vals = [v(w) for _, v in sources for w in range(tiles + 1)]
    raw = scores_of(query, jnp.concatenate(keys, axis=0))
    blocks = []
    for u in range(tiles):
        line = []
        for i in range(len(keys)):
            w = i % (tiles + 1)
            block = raw[u * tile_len : (u + 1) * tile_len, i * tile_len : (i + 1) * tile_len]
            if w == tiles:
                sides = [side for side, end in ((1, 0), (0, tiles - 1)) if u == end]
                if not sides:
                    block = None
                else:
                    block = block + jnp.where(row_pos == sides[0], zero, neg)
            elif abs(w - u) > 1:
                block = None
            line.append(block)
        blocks.append(line)
    return blocks, vals


def weights_of(line, old_top, factor):
    live = [block for block in line if block is not None]
    top = jnp.max(functools.reduce(jnp.maximum, live), axis=1, keepdims=True)
    if old_top is not None:
        top = jnp.maximum(old_top, top)
    shift = top * factor
    weights = [None if b is None else jnp.exp2(b * factor - shift) for b in line]
    total = functools.reduce(jnp.add, [w for w in weights if w is not None])
    total = jnp.sum(total, axis=1, keepdims=True)
    blank = jnp.zeros(live[0].shape, jnp.bfloat16)
    rounded = [blank if w is None else w.astype(jnp.bfloat16) for w in weights]
    return top, total, jnp.concatenate(rounded, axis=1)


def product(weights, vals):
    return jnp.dot(weights, jnp.concatenate(vals, axis=0), preferred_element_type=jnp.float32)


def near_kernel(
    plan, reach, device, valid, q_ref, k_ref, v_ref, edge_ref, hk_ref, hv_ref, sk_ref, sv_ref,
    acc_ref, top_ref, sum_ref, *, factor
):
    head = pl.program_id(0)
    tiles, tile_len, _ = q_ref.shape
    row_pos = device[0] % ROW_BLOCKS
    lanes = lax.broadcasted_iota(jnp.int32, (tile_len, top_ref.shape[-1]), 1)
    local = (
        lambda w: k_ref[w] if w < tiles else edge_ref[0],
        lambda w: v_ref[w] if w < tiles else edge_ref[1],
    )
    timed = (
        lambda w: hk_ref[0, w] if w < tiles else sk_ref[0],
        lambda w: hv_ref[0, w] if w < tiles else sv_ref[0],
    )

    def run(sources, rows):
        blocks, vals = window_blocks(sources, rows, q_ref, slice(None), row_pos)
        parts = [weights_of(line, None, factor) for line in blocks]
        if rows:
            mixed = product(jnp.concatenate([p[2] for p in parts], axis=0), vals)
            mixed = [mixed[u * tile_len : (u + 1) * tile_len] for u in range(tiles)]
        else:
            mixed = [product(parts[u][2], vals[u]) for u in range(tiles)]
        for u in range(tiles):
            acc_ref[u] = mixed[u]
            top_ref[u] = jnp.where(lanes == head, parts[u][0], top_ref[u])
            sum_ref[u] = jnp.where(lanes == head, parts[u][1], sum_ref[u])

    with_time = (plan[7, head] > 0) & (valid[0] > 0)
    for rows in (0, 1):
        for time in (0, 1):
            pl.when((with_time == bool(time)) & ((reach[head] > 0) == bool(rows)))(
                functools.partial(run, (local, timed) if time else (local,), rows)
            )


def column_of(ref, u, lanes, head):
    return jnp.sum(jnp.where(lanes == head, ref[u], jnp.float32(0)), axis=1, keepdims=True)


def time_kernel(
    plan, reach, device, valid, q_ref, hk_ref, hv_ref, sk_ref, sv_ref, acc_ref, top_ref, sum_ref,
    _, out_ref, *, factor
):
    slot = pl.program_id(0)
    head = plan[3, slot]
    tiles, tile_len, _ = q_ref.shape
    row_pos = device[0] % ROW_BLOCKS
    lanes = lax.broadcasted_iota(jnp.int32, (tile_len, top_ref.shape[-1]), 1)
    source = (
        lambda w: hk_ref[0, w] if w < tiles else sk_ref[0],
        lambda w: hv_ref[0, w] if w < tiles else sv_ref[0],
    )

    def run(rows):
        blocks, vals = window_blocks((source,), rows, q_ref, slice(None), row_pos)
        tops = [column_of(top_ref, u, lanes, head) for u in range(tiles)]
        parts = [weights_of(blocks[u], tops[u], factor) for u in range(tiles)]
        if rows:
            mixed = product(jnp.concatenate([p[2] for p in parts], axis=0), vals)
            mixed = [mixed[u * tile_len : (u + 1) * tile_len] for u in range(tiles)]
        else:
            mixed = [product(parts[u][2], vals[u]) for u in range(tiles)]
        for u in range(tiles):
            top, total, _ = parts[u]
            keep = jnp.exp2(tops[u] * factor - top * factor)
            total = keep * column_of(sum_ref, u, lanes, head) + total
            out_ref[u] = ((acc_ref[u] * keep + mixed[u]) / total).astype(out_ref.dtype)

    count = plan[4, 0]
    go = (slot < count) & (valid[0] > 0)
    for rows in (0, 1):
        pl.when(go & ((reach[head] > 0) == bool(rows)))(functools.partial(run, rows))

    @pl.when(jnp.logical_not(go) & ((slot < count) | (slot == 0)))
    def _():
        for u in range(tiles):
            out_ref[u] = (acc_ref[u] / column_of(sum_ref, u, lanes, head)).astype(out_ref.dtype)


def far_kernel(plan, q_ref, acc_ref, top_ref, sum_ref, *refs, factor):
    fars, (out_ref, acc_out, top_out, sum_out) = refs[:-4], refs[-4:]
    step = pl.program_id(0)
    tiles, tile_len, _ = q_ref.shape
    width = out_ref.shape[-1] // len(fars)
    neg, zero = jnp.float32(BIG_NEG), jnp.float32(0)
    lanes = lax.broadcasted_iota(jnp.int32, (tile_len, top_ref.shape[-1]), 1)
    for g, far_ref in enumerate(fars):
        head = step * len(fars) + g
        at = slice(g * width, (g + 1) * width)
        word = plan[2, head]
        query = jnp.concatenate([q_ref[u, :, at] for u in range(tiles)], axis=0)
        raw = scores_of(query, jnp.concatenate([far_ref[0, 0, i] for i in range(LIST)], axis=0))
        lines = []
        for u in range(tiles):
            line = []
            for i in range(LIST):
                live = (word // (1 << (u * LIST + i))) % 2
                block = raw[u * tile_len : (u + 1) * tile_len, i * tile_len : (i + 1) * tile_len]
                line.append(block + jnp.where(live > 0, zero, neg))
            lines.append(line)
        tops = [column_of(top_ref, u, lanes, head) for u in range(tiles)]
        parts = [weights_of(lines[u], tops[u], factor) for u in range(tiles)]
        mixed = product(
            jnp.concatenate([p[2] for p in parts], axis=0), [far_ref[0, 1, i] for i in range(LIST)]
        )
        for u in range(tiles):
            top, total, _ = parts[u]
            keep = jnp.exp2(tops[u] * factor - top * factor)
            total = keep * column_of(sum_ref, u, lanes, head) + total
            whole = acc_ref[u, :, at] * keep + mixed[u * tile_len : (u + 1) * tile_len]
            out_ref[u, :, at] = (whole / total).astype(out_ref.dtype)
            acc_out[u, :, at] = whole
            top_out[u] = jnp.where(lanes == head, top, top_out[u])
            sum_out[u] = jnp.where(lanes == head, total, sum_out[u])


def any_spec():
    return pl.BlockSpec(memory_space=pl.ANY)


def smem_spec():
    return pl.BlockSpec(memory_space=pltpu.SMEM)


def vmem_spec():
    return pl.BlockSpec(memory_space=pltpu.VMEM)


def on_device(relay, queries, keys, values, block_list, list_len, window_time, window_rows):
    tiles, tile_len, feat = queries.shape
    heads = window_time.shape[0]
    width = feat // heads
    blocks = lax.axis_size("seq")
    axis = lax.axis_index("seq").astype(jnp.int32)
    device = axis.reshape(1)
    time_block = axis // ROW_BLOCKS
    row_pos = axis % ROW_BLOCKS
    time_blocks = blocks // ROW_BLOCKS
    dtype = keys.dtype
    factor = math.log2(math.e) / math.sqrt(width)
    timed_count = jnp.sum((window_time > 0).astype(jnp.int32))
    side = jnp.where(row_pos == 0, tiles - 1, 0)
    if relay:
        first_ok = jnp.int32(1)
        second_ok = jnp.where(time_block % 2 == 0, time_block > 0, time_block < time_blocks - 1)
    else:
        first_ok = time_block > 0
        second_ok = time_block < time_blocks - 1
    oks = [ok.astype(jnp.int32).reshape(1) for ok in (first_ok, second_ok)]
    lists = jnp.transpose(block_list, (1, 2, 0))
    lens = jnp.transpose(list_len, (1, 0))
    per_source = (heads + blocks - 2) // (blocks - 1)
    slots = per_source * LIST
    pair_tile = tile_len * width * 2
    lanes = -(-lists.shape[2] // 128) * 128
    sublanes = -(-heads // 8) * 8
    pair_route = [(i, i ^ 1) for i in range(blocks)]

    def permute(value, route):
        return lax.ppermute(value, "seq", route)

    def at_head(h, *_):
        return (0, 0, h)

    tile_spec = pl.BlockSpec((tiles, tile_len, width), at_head)

    def near(cap):
        return near_of(cap)

    def near_of(cap):
        halo_shape = jax.ShapeDtypeStruct((cap, tiles, tile_len, width), dtype)
        halo_key, halo_val, edge, far, plan = pl.pallas_call(
            pack_kernel,
            out_shape=(
                halo_shape,
                halo_shape,
                jax.ShapeDtypeStruct((2, tile_len, feat), dtype),
                jax.ShapeDtypeStruct((blocks, 2, slots, tile_len, width), dtype),
                jax.ShapeDtypeStruct((8, 128), jnp.int32),
            ),
            in_specs=[smem_spec(), smem_spec(), vmem_spec(), vmem_spec(), smem_spec(), smem_spec()]
            + [any_spec()] * 2,
            out_specs=[any_spec()] * 4 + [smem_spec()],
            scratch_shapes=[
                pltpu.VMEM(keys.shape, dtype),
                pltpu.VMEM(values.shape, dtype),
                pltpu.VMEM((2, sublanes, lanes), jnp.int32),
                pltpu.VMEM((8, lanes), jnp.int32),
                pltpu.SMEM((8, lanes), jnp.int32),
                pltpu.SemaphoreType.DMA((2,)),
                pltpu.SemaphoreType.DMA((4,)),
                pltpu.SemaphoreType.DMA,
            ],
            cost_estimate=pl.CostEstimate(
                flops=0,
                transcendentals=0,
                bytes_accessed=(2 * blocks * slots + 6 * cap) * pair_tile,
            ),
            name="pack",
        )(window_time, device, lists, lens, lists, lens, keys, values)

        if relay:
            step = 2 * ROW_BLOCKS
            one_hop = [(i, i ^ ROW_BLOCKS) for i in range(blocks)]
            other = []
            for i in range(blocks):
                to = i + step if (i // ROW_BLOCKS) % 2 == 0 else i - step
                if 0 <= to < blocks:
                    other.append((i, to))
            straight = []
            for i in range(blocks):
                to = i - ROW_BLOCKS if (i // ROW_BLOCKS) % 2 == 0 else i + ROW_BLOCKS
                if 0 <= to < blocks:
                    straight.append((i, to))
            first_key = permute(halo_key, one_hop)
            first_val = permute(halo_val, one_hop)
            first = [first_key, first_val]
            second_key = permute(first_key, other)
            second_val = permute(halo_val, straight)
            second = [second_key, second_val]
        else:
            step = ROW_BLOCKS
            after = [(i, i + step) for i in range(blocks - step)]
            ahead = [(i + step, i) for i in range(blocks - step)]
            first_key = permute(halo_key, after)
            first_val = permute(halo_val, after)
            first = [first_key, first_val]
            second_key = permute(halo_key, ahead)
            second_val = permute(halo_val, ahead)
            second = [second_key, second_val]
        far = lax.all_to_all(far, "seq", split_axis=0, concat_axis=0, tiled=True)
        edge = permute(edge, pair_route)

        def side_of(value):
            return permute(lax.dynamic_index_in_dim(value, side, 1, keepdims=False), pair_route)

        halves = [(*halo, *[side_of(x) for x in halo]) for halo in (first, second)]

        def halo_specs(at):
            def whole(s, plan_ref, *_):
                return (plan_ref[6, at(s)], 0, 0, 0)

            def part(s, plan_ref, *_):
                return (plan_ref[6, at(s)], 0, 0)

            return [pl.BlockSpec((1, tiles, tile_len, width), whole)] * 2 + [
                pl.BlockSpec((1, tile_len, width), part)
            ] * 2

        stat_spec = pl.BlockSpec((tiles, tile_len, 128), lambda h, *_: (0, 0, 0))
        stat_shape = jax.ShapeDtypeStruct((tiles, tile_len, 128), jnp.float32)
        pairs = (heads + cap) * tiles * 2
        state = pl.pallas_call(
            functools.partial(near_kernel, factor=factor),
            grid_spec=pltpu.PrefetchScalarGridSpec(
                num_scalar_prefetch=4,
                grid=(heads,),
                in_specs=[tile_spec] * 3
                + [pl.BlockSpec((2, tile_len, width), at_head)]
                + halo_specs(lambda s: s),
                out_specs=[tile_spec, stat_spec, stat_spec],
            ),
            out_shape=(
                jax.ShapeDtypeStruct((tiles, tile_len, feat), jnp.float32),
                stat_shape,
                stat_shape,
            ),
            cost_estimate=pl.CostEstimate(
                flops=pairs * 4 * tile_len * tile_len * width,
                transcendentals=pairs * tile_len * tile_len,
                bytes_accessed=8 * tiles * tile_len * feat * 2,
            ),
            name="near",
        )(plan, window_rows, device, oks[0], queries, keys, values, edge, *halves[0])

        group = GROUP if heads % GROUP == 0 else 1
        wide_spec = pl.BlockSpec((tiles, tile_len, width * group), at_head)

        def far_spec(g):
            return pl.BlockSpec(
                (1, 2, LIST, tile_len, width),
                lambda s, p: (p[0, s * group + g], 0, p[1, s * group + g], 0, 0),
            )

        acc_shape = jax.ShapeDtypeStruct((tiles, tile_len, feat), jnp.float32)
        pairs = heads * tiles * LIST
        out, *state = pl.pallas_call(
            functools.partial(far_kernel, factor=factor),
            grid_spec=pltpu.PrefetchScalarGridSpec(
                num_scalar_prefetch=1,
                grid=(heads // group,),
                in_specs=[wide_spec] * 2
                + [stat_spec] * 2
                + [far_spec(g) for g in range(group)],
                out_specs=[wide_spec] * 2 + [stat_spec] * 2,
            ),
            out_shape=(
                jax.ShapeDtypeStruct(queries.shape, queries.dtype),
                acc_shape,
                stat_shape,
                stat_shape,
            ),
            cost_estimate=pl.CostEstimate(
                flops=pairs * 4 * tile_len * tile_len * width,
                transcendentals=pairs * tile_len * tile_len,
                bytes_accessed=8 * tiles * tile_len * feat * 2,
            ),
            name="far",
        )(plan, queries, *state, *([far] * group))

        def at_plan(s, plan_ref, *_):
            return (0, 0, plan_ref[3, s])

        planned = pl.BlockSpec((tiles, tile_len, width), at_plan)
        halo_spec = pl.BlockSpec((1, tiles, tile_len, width), lambda s, *_: (s, 0, 0, 0))
        side_spec = pl.BlockSpec((1, tile_len, width), lambda s, *_: (s, 0, 0))
        pairs = cap * tiles * 3
        return pl.pallas_call(
            functools.partial(time_kernel, factor=factor),
            grid_spec=pltpu.PrefetchScalarGridSpec(
                num_scalar_prefetch=4,
                grid=(cap,),
                in_specs=[
                    planned,
                    halo_spec,
                    halo_spec,
                    side_spec,
                    side_spec,
                    planned,
                    stat_spec,
                    stat_spec,
                    any_spec(),
                ],
                out_specs=planned,
            ),
            out_shape=jax.ShapeDtypeStruct(queries.shape, queries.dtype),
            input_output_aliases={12: 0},
            cost_estimate=pl.CostEstimate(
                flops=pairs * 4 * tile_len * tile_len * width,
                transcendentals=pairs * tile_len * tile_len,
                bytes_accessed=8 * cap * tiles * pair_tile,
            ),
            name="time",
        )(plan, window_rows, device, oks[1], queries, *halves[1], *state, out)

    caps = [c for c in CAPS if c < heads] + [heads]
    pick = sum((timed_count > c).astype(jnp.int32) for c in caps[:-1])
    return lax.switch(pick, [functools.partial(near, c) for c in caps])


def solution(mesh):
    return jax.shard_map(
            functools.partial(on_device, relay_fits(mesh)),
            mesh=mesh,
            in_specs=(
                P(("group", "seq"), None, None),
                P(("group", "seq"), None, None),
                P(("group", "seq"), None, None),
                P("group", None, None),
                P("group", None),
                P(),
                P(),
            ),
            out_specs=P(("group", "seq"), None, None),
            check_vma=False,
    )
```
